512 devices in a mesh: alpha: 16 (over x, z_hi), beta: 32 (over z_lo, y, core).
Axes of the slice: x: 4, y: 8, z: 8 (z_hi: 4, z_lo: 2; z = z_hi * 2 + z_lo), core: 2. Of those that a mesh axis runs over, the one named last changes fastest.
Arguments:
- amplitudes: float32 [12288, 12288], P('alpha', 'beta'), may hold values from -6 to 6
- coupled_index: int32 [96, 16], P('beta'), may hold values from 0 to 95, as said below
- coupling_blocks: bfloat16 [96, 16, 128, 128], P('beta'), may hold values from -0.125 to 0.125
- string_energy: float32 [12288], replicated, may hold values from -1 to 1
- shift_index: int32 [2], replicated, may hold values from 0 to 12287
Outputs:
- refined: float32 [12288, 12288], P('alpha', 'beta')
The draws below stay inside these ranges and needn't reach their ends.
Inputs may be any that keep to these rules, and one draw needn't show every extreme that they name: `coupled_index`: row J holds 16 different blocks, each (J + d) mod 96 for some d with |d| <= 9.
All inputs are finite; a program needn't handle non-finite values.
Results may differ from the reference program's by a relative error of at most 0.0035.
Values may be sent and summed in bfloat16 or wider, within the bound.
A program may use at most 64 MiB of HBM per device.

```python
import jax
import jax.numpy as jnp
from jax import lax

BLK = 128
COUPLE = 16
REACH = 9
STEPS = 2
STRINGS = 12288
NBLK = 96


def draw_coupled_index(key, part):
    span = 2 * REACH + 1
    scores = jax.random.randint(key, (NBLK, span), 0, 1 << 20) * span + jnp.arange(span, dtype=jnp.int32)[None, :]
    order = jnp.argsort(scores, axis=1, stable=True)[:, :COUPLE].astype(jnp.int32)
    offset = order - REACH
    return ((jnp.arange(NBLK, dtype=jnp.int32)[:, None] + offset) % NBLK).astype(jnp.int32)


def shard_levels(stream_key, dims, split, low, high):
    factor_of, own = 1.0, jax.random.fold_in(stream_key, 6)
    for position, blocks in split:
        draws = jnp.exp(jax.random.uniform(jax.random.fold_in(own, position), (blocks,), jnp.float32, low / len(split), high / len(split)))
        factor_of = factor_of * jnp.repeat(draws, dims[position] // blocks).reshape([-1 if axis == position else 1 for axis in range(len(dims))])
    return factor_of


def centred(stream_key, extent, scale, reach, pieces=(), kind=jnp.bfloat16):
    entries = jax.random.normal(stream_key, extent, jnp.float32) * scale
    if len(pieces) > 0:
        entries = shard_levels(stream_key, extent, pieces, -0.22, 0.18) * entries
    return jnp.clip(entries, min=-reach, max=reach).astype(kind)


def setup_inputs(seed: int = 0) -> dict:
    key_list = jax.random.split(jax.random.key(seed), 6)
    return {
        "amplitudes": centred(key_list[0], (STRINGS, STRINGS), 1.0, 6.0, ((0, 16), (1, 32)), jnp.float32),
        "coupled_index": draw_coupled_index(jax.random.fold_in(key_list[5], 71), 0),
        "coupling_blocks": centred(key_list[2], (NBLK, COUPLE, BLK, BLK), (COUPLE * BLK) ** -0.5, 0.125, ((0, 32),)),
        "string_energy": jnp.clip(jax.random.uniform(key_list[3], (STRINGS,), jnp.float32, -1.0, 1.0), -1.0, 1.0),
        "shift_index": jax.random.randint(key_list[4], (STEPS,), 0, STRINGS).astype(jnp.int32),
    }


def reference(amplitudes, coupled_index, coupling_blocks, string_energy, shift_index):
    strings = amplitudes.shape[0]
    blocks = strings // BLK
    current = amplitudes
    for iteration in range(STEPS):
        rounded = current.astype(jnp.bfloat16)
        grouped = rounded.reshape(strings, blocks, BLK)

        def block_column(packed):
            listed, weights = packed
            picked = jnp.take(grouped, listed, axis=1).astype(jnp.float32).reshape(strings, COUPLE * BLK)
            flat_weights = weights.astype(jnp.float32).reshape(COUPLE * BLK, BLK)
            return jnp.dot(picked, flat_weights, preferred_element_type=jnp.float32)

        columns = lax.map(block_column, (coupled_index, coupling_blocks))
        mixed = jnp.transpose(columns, (1, 0, 2)).reshape(strings, strings).astype(jnp.bfloat16)
        widened = mixed.astype(jnp.float32)
        sigma = widened + widened.T
        shift = 2.0 * string_energy[shift_index[iteration]]
        residual = sigma - shift * current
        gap = string_energy[:, None] + string_energy[None, :] - shift
        current = current - residual * gap / (gap * gap + 1.0)
    return current
```

```python
import functools

import jax
import jax.numpy as jnp
from jax import lax
from jax.experimental import pallas as pl
from jax.experimental.pallas import tpu as pltpu
from jax.sharding import PartitionSpec as P

BLK = 128
REACH = 9
STEPS = 2
HOPS = 3
TILES = 2 * HOPS + 1
CHUNKS = 6
SPREAD = 8
MESH = pl.DeviceIdType.MESH


def kernel(
    amp_hbm, idx_ref, coup_hbm, energy_ref, shift_ref, out_ref,
    cur, halo, coup, banded, weight, mixed, inter, fin, pos_ref,
    load_sem, coup_sem, hsend, hrecv, leg1_send, leg1_recv, leg2_send, leg2_recv,
):
    rows, cols = amp_hbm.shape
    chunk_rows = rows // CHUNKS
    half = rows // 2
    piece = half // SPREAD
    blocks = cols // BLK
    couple = coup_hbm.shape[1]
    alpha = lax.axis_index("alpha")
    beta = lax.axis_index("beta")
    chip = beta // 2
    core = beta % 2
    chips = lax.axis_size("beta") // 2
    right = 2 * ((chip + 1) % chips)
    left = 2 * ((chip + chips - 1) % chips)
    sibling = 2 * chip + 1 - core
    far = 2 * ((chip + chips + 2 * core - 1) % chips) + 1 - core
    beta_group = beta // (2 * SPREAD)
    own_place = chip % SPREAD

    def load(i):
        at = pl.ds(i * chunk_rows, chunk_rows)
        return pltpu.make_async_copy(amp_hbm.at[at], cur.at[at], load_sem.at[i])

    def coup_copy():
        return pltpu.make_async_copy(coup_hbm, coup.at[pl.ds(0, blocks)], coup_sem)

    for i in range(CHUNKS):
        load(i).start()
    coup_copy().start()

    def remote(step, kind, i, src_slot, dst_slot, to):
        at = pl.ds(pl.multiple_of(i * chunk_rows, chunk_rows), chunk_rows)
        return pltpu.make_async_remote_copy(
            halo.at[step, src_slot, at],
            halo.at[step, dst_slot, at],
            hsend.at[step, kind, i],
            hrecv.at[step, kind, i],
            device_id=(alpha, to),
            device_id_type=MESH,
        )

    def to_right(step, i):
        return remote(step, 0, i, 3, 1, right + core)

    def to_left(step, i):
        return remote(step, 1, i, 3, 5, left + core)

    def to_sibling(step, i):
        return remote(step, 2, i, 3, 2 * core + 2, sibling)

    def pass_left_tile(step, i):
        return remote(step, 3, i, 1, 2 * core, sibling)

    def pass_right_tile(step, i):
        return remote(step, 4, i, 5, 2 * core + 4, sibling)

    def pass_far(step, i):
        return remote(step, 5, i, 5 - 4 * core, 6 - 6 * core, far)

    halo_kinds = (to_right, to_left, to_sibling, pass_left_tile, pass_right_tile, pass_far)

    def start_own(step, i):
        to_right(step, i).start()
        to_left(step, i).start()
        to_sibling(step, i).start()

    for i in range(CHUNKS):
        load(i).wait()
        at = pl.ds(i * chunk_rows, chunk_rows)
        halo[0, HOPS, at, :] = cur[at, :].astype(jnp.bfloat16)
        start_own(0, i)

    coup_copy().wait()
    coup[blocks, 0] = jnp.zeros((BLK, BLK), jnp.bfloat16)
    total = blocks * lax.axis_size("beta")
    for j in range(blocks):
        mine = beta * blocks + j
        for t in range(couple):
            offset = (idx_ref[j, t] - mine + REACH + total) % total - REACH
            pos_ref[j, t] = HOPS * blocks + j + offset

    def build(slot, carry):
        for u in range(blocks):
            place = slot * blocks + u
            for j in range(blocks):
                found_j = blocks
                found_t = 0
                for t in range(couple):
                    hit = pos_ref[j, t] == place
                    found_j = jnp.where(hit, j, found_j)
                    found_t = jnp.where(hit, t, found_t)
                banded[slot, pl.ds(u * BLK, BLK), pl.ds(j * BLK, BLK)] = coup[found_j, found_t]
        return carry

    lax.fori_loop(0, TILES, build, 0)

    places = lax.broadcasted_iota(jnp.int32, energy_ref.shape, 0) * BLK + lax.broadcasted_iota(
        jnp.int32, energy_ref.shape, 1
    )

    def shift_of(step):
        chosen = jnp.where(places == shift_ref[step], energy_ref[...], 0.0)
        return 2.0 * jnp.sum(chosen)

    row_blocks = rows // BLK

    def fill_weight(step, shift):
        def body(i, carry):
            row_line = energy_ref[pl.ds(alpha * row_blocks + i, 1), :]
            column = jnp.transpose(jnp.broadcast_to(row_line, (BLK, BLK)))
            at = pl.ds(pl.multiple_of(i * BLK, BLK), BLK)
            for j in range(blocks):
                gap = column + energy_ref[pl.ds(beta * blocks + j, 1), :] - shift
                weight[at, pl.ds(j * BLK, BLK)] = gap / (gap * gap + 1.0)
            return carry

        lax.fori_loop(0, row_blocks, body, 0)

    diagonal = (alpha == chip)

    def leg1(step, i):
        place = (own_place + i) % SPREAD
        return pltpu.make_async_remote_copy(
            mixed.at[step, :, i],
            inter.at[step, alpha % SPREAD],
            leg1_send.at[step, i],
            leg1_recv.at[step, alpha % SPREAD],
            device_id=(chip, (alpha // SPREAD) * 2 * SPREAD + 2 * place + core),
            device_id_type=MESH,
        )

    def leg1_self(step):
        return pltpu.make_async_copy(
            mixed.at[step, :, 0],
            inter.at[step, alpha % SPREAD],
            leg1_recv.at[step, alpha % SPREAD],
        )

    source_piece = (own_place + SPREAD - alpha % SPREAD) % SPREAD

    def leg1_arrived(step, m):
        return pltpu.make_async_copy(
            inter.at[step, m], inter.at[step, m], leg1_recv.at[step, m]
        )

    def leg2(step, m, to_core):
        return pltpu.make_async_remote_copy(
            inter.at[step, m, to_core],
            fin.at[step, core, source_piece],
            leg2_send.at[step, m, to_core],
            leg2_recv.at[step, core],
            device_id=(alpha, beta_group * 2 * SPREAD + 2 * m + to_core),
            device_id_type=MESH,
        )

    def leg2_self(step):
        return pltpu.make_async_copy(
            inter.at[step, own_place, core],
            fin.at[step, core, source_piece],
            leg2_recv.at[step, core],
        )

    for step in range(STEPS):
        shift = shift_of(step)
        fill_weight(step, shift)

        def forward(i, carry):
            to_right(step, i).wait_recv()
            pass_left_tile(step, i).start()
            to_left(step, i).wait_recv()
            pass_right_tile(step, i).start()
            pass_far(step, i).start()
            return carry

        lax.fori_loop(0, CHUNKS, forward, 0)

        pieces_per_chunk = chunk_rows // piece if chunk_rows >= piece else 1

        def mix(i, carry):
            for copy in halo_kinds[2:]:
                copy(step, i).wait_recv()
            at = pl.ds(pl.multiple_of(i * chunk_rows, chunk_rows), chunk_rows)
            acc = jnp.dot(halo[step, 0, at, :], banded[0], preferred_element_type=jnp.float32)
            for slot in range(1, TILES):
                acc = acc + jnp.dot(
                    halo[step, slot, at, :], banded[slot], preferred_element_type=jnp.float32
                )
            low = acc.astype(jnp.bfloat16)
            per_half = CHUNKS // 2
            flat = mixed.at[step, i // per_half]
            base = (i % per_half) * chunk_rows
            for q in range(chunk_rows // 16):
                start = base + q * 16
                flat[start // piece, pl.ds(pl.multiple_of(start % piece, 16), 16), :] = low[
                    q * 16 : (q + 1) * 16
                ]
            wide = low.astype(jnp.float32)
            factor = weight[at, :]
            cur[at, :] = cur[at, :] * (1.0 + shift * factor) - wide * factor
            return carry

        lax.fori_loop(0, CHUNKS, mix, 0)

        for i in range(SPREAD):
            if i == 0:
                pl.when(diagonal)(leg1_self(step).start)
                pl.when(jnp.logical_not(diagonal))(leg1(step, i).start)
            else:
                leg1(step, i).start()

        def onward(d, carry):
            m = (own_place + d) % SPREAD
            leg1_arrived(step, m).wait()
            leg2(step, m, 0).start()
            leg2(step, m, 1).start()
            return carry

        lax.fori_loop(1, SPREAD, onward, 0)
        leg1_arrived(step, own_place).wait()
        leg2(step, own_place, 1 - core).start()
        leg2_self(step).start()

        for copy in halo_kinds:
            for i in range(CHUNKS):
                copy(step, i).wait_send()
        for i in range(SPREAD):
            if i == 0:
                pl.when(jnp.logical_not(diagonal))(leg1(step, i).wait_send)
            else:
                leg1(step, i).wait_send()

        per_half = CHUNKS // 2
        for c in range(2):
            pltpu.make_async_copy(fin.at[step, c], fin.at[step, c], leg2_recv.at[step, c]).wait()
            for k in range(blocks):
                row = c * half + k * BLK
                for j in range(blocks):
                    lines = []
                    for q in range(BLK // 16):
                        start = j * BLK + q * 16
                        lines.append(
                            fin[step, c, start // piece, pl.ds(start % piece, 16), pl.ds(k * BLK, BLK)]
                        )
                    block = jnp.concatenate(lines, axis=0).astype(jnp.float32)
                    mirror = jnp.transpose(block)
                    at = (pl.ds(row, BLK), pl.ds(j * BLK, BLK))
                    fresh = cur[at] - mirror * weight[at]
                    if step < STEPS - 1:
                        cur[at] = fresh
                        halo[step + 1, HOPS, pl.ds(row, BLK), pl.ds(j * BLK, BLK)] = fresh.astype(
                            jnp.bfloat16
                        )
                    else:
                        out_ref[at] = fresh
                if step < STEPS - 1:
                    start_own(step + 1, row // chunk_rows)

        def drain(d, carry):
            m = (own_place + d) % SPREAD
            leg2(step, m, 0).wait_send()
            leg2(step, m, 1).wait_send()
            return carry

        lax.fori_loop(1, SPREAD, drain, 0)
        leg2(step, own_place, 1 - core).wait_send()


def local(amplitudes, coupled_index, coupling_blocks, string_energy, shift_index):
    rows, cols = amplitudes.shape
    blocks = coupled_index.shape[0]
    couple = coupled_index.shape[1]
    half = rows // 2
    piece = half // SPREAD
    energy = string_energy.reshape(-1, BLK)
    any_space = pl.BlockSpec(memory_space=pl.ANY)
    vmem = pl.BlockSpec(memory_space=pltpu.VMEM)
    smem = pl.BlockSpec(memory_space=pltpu.SMEM)
    dma = pltpu.SemaphoreType.DMA
    return pl.pallas_call(
        kernel,
        out_shape=jax.ShapeDtypeStruct((rows, cols), jnp.float32),
        in_specs=[any_space, smem, any_space, vmem, smem],
        out_specs=vmem,
        scratch_shapes=[
            pltpu.VMEM((rows, cols), jnp.float32),
            pltpu.VMEM((STEPS, TILES, rows, cols), jnp.bfloat16),
            pltpu.VMEM((blocks + 1, couple, BLK, BLK), jnp.bfloat16),
            pltpu.VMEM((TILES, cols, cols), jnp.bfloat16),
            pltpu.VMEM((rows, cols), jnp.float32),
            pltpu.VMEM((STEPS, 2, SPREAD, piece, cols), jnp.bfloat16),
            pltpu.VMEM((STEPS, SPREAD, 2, piece, cols), jnp.bfloat16),
            pltpu.VMEM((STEPS, 2, SPREAD, piece, cols), jnp.bfloat16),
            pltpu.SMEM((blocks, couple), jnp.int32),
            dma((CHUNKS,)),
            dma,
            dma((STEPS, 6, CHUNKS)),
            dma((STEPS, 6, CHUNKS)),
            dma((STEPS, SPREAD)),
            dma((STEPS, SPREAD)),
            dma((STEPS, SPREAD, 2)),
            dma((STEPS, 2)),
        ],
        compiler_params=pltpu.CompilerParams(
            has_side_effects=True, vmem_limit_bytes=48 * 1024 * 1024
        ),
        cost_estimate=pl.CostEstimate(
            flops=2 * STEPS * TILES * rows * cols * cols, bytes_accessed=8 << 20, transcendentals=0
        ),
        name="residual_steps",
    )(amplitudes, coupled_index, coupling_blocks, energy, shift_index)


def solution(mesh):
    placed = (P("alpha", "beta"), P("beta", None), P("beta", None, None, None), P(), P())
    return jax.shard_map(
        local, mesh=mesh, in_specs=placed, out_specs=P("alpha", "beta"), check_vma=False
    )
```

```python
import jax
import jax.numpy as jnp
from jax import lax
from jax.experimental import pallas as pl
from jax.experimental.pallas import tpu as pltpu
from jax.sharding import PartitionSpec as P

BLK = 128
REACH = 9
STEPS = 2
HOPS = 3
TILES = 2 * HOPS + 1
CHUNKS = 6
SPREAD = 8
MESH = pl.DeviceIdType.MESH
ROUTES = (
    (),
    (64, 80, 192, 192, 1, 16, 17, 17),
    (176, 89, 80, 122, 248, 24, 40, 40),
    (168, 178, 128, 58, 240, 49, 48, 51),
    (133, 192, 193, 193, 3, 4, 7, 67),
    (146, 151, 211, 22, 16, 80, 80, 85),
    (152, 152, 174, 232, 248, 248, 40, 56),
    (88, 114, 128, 128, 199, 120, 48, 55),
    (64, 64, 128, 128, 128, 192, 192, 200),
    (30, 16, 1, 24, 64, 88, 128, 192),
    (112, 144, 216, 233, 40, 104, 106, 170),
    (255, 58, 64, 120, 131, 192, 192, 248),
    (73, 74, 129, 142, 4, 5, 198, 202),
    (168, 154, 222, 5, 192, 192, 216, 216),
    (80, 184, 128, 208, 233, 6, 40, 198),
    (186, 71, 120, 57, 56, 63, 192, 248),
)


def inbound_routes():
    found = [[] for _ in ROUTES]
    slots = {}
    for piece in range(SPREAD):
        for kind, row in enumerate(ROUTES):
            if row:
                at = kind ^ (row[piece] // 16) ^ (row[piece] % 16)
                slots[kind, piece] = len(found[at])
                found[at].append((row[piece], piece))
    return found, slots


INBOUND, SLOTS = inbound_routes()
INSLOTS = max(len(entries) for entries in INBOUND)


def kernel(
    amp_hbm, idx_ref, coup_hbm, energy_ref, shift_ref, out_ref,
    cur, halo, coup, banded, weight, mixed, inter, fin, pos_ref,
    load_sem, coup_sem, hsend, hrecv, leg1_send, leg1_recv, leg2_send, leg2_recv,
):
    rows, cols = amp_hbm.shape
    chunk_rows = rows // CHUNKS
    half = rows // 2
    piece = half // SPREAD
    blocks = cols // BLK
    couple = coup_hbm.shape[1]
    alpha = lax.axis_index("alpha")
    beta = lax.axis_index("beta")
    chip = beta // 2
    core = beta % 2
    chips = lax.axis_size("beta") // 2
    right = 2 * ((chip + 1) % chips)
    left = 2 * ((chip + chips - 1) % chips)
    sibling = 2 * chip + 1 - core
    far = 2 * ((chip + chips + 2 * core - 1) % chips) + 1 - core

    def load(i):
        at = pl.ds(i * chunk_rows, chunk_rows)
        return pltpu.make_async_copy(amp_hbm.at[at], cur.at[at], load_sem.at[i])

    def coup_copy():
        return pltpu.make_async_copy(coup_hbm, coup.at[pl.ds(0, blocks)], coup_sem)

    for i in range(CHUNKS):
        load(i).start()
    coup_copy().start()

    def bits(value):
        return [(value // 2**k) % 2 for k in range(4)]

    alpha_bits, chip_bits = bits(alpha), bits(chip)
    kind = sum((p + q) % 2 * 2**k for k, (p, q) in enumerate(zip(alpha_bits, chip_bits)))
    stays = kind == 0

    def pick(values):
        chosen = jnp.int32(values[0])
        for k in range(1, len(ROUTES)):
            if values[k] != values[0]:
                chosen = jnp.where(kind == k, values[k], chosen)
        return chosen

    def flipped(base, base_bits, flips):
        for k in range(4):
            base = base + (flips // 2**k) % 2 * (2**k * (1 - 2 * base_bits[k]))
        return base

    outs = []
    back = []
    for p in range(SPREAD):
        route = pick([row[p] if row else 0 for row in ROUTES])
        slot = pick([SLOTS.get((k, p), 0) for k in range(len(ROUTES))])
        through = flipped(alpha, alpha_bits, route // 16)
        outs.append((through, 2 * flipped(chip, chip_bits, route % 16) + core, slot))
        back.append((flipped(chip, chip_bits, route // 16), flipped(alpha, alpha_bits, route % 16)))
    ins = []
    for n in range(INSLOTS):
        entries = [row[n] if n < len(row) else (0, 0) for row in INBOUND]
        counts = [n < len(row) for row in INBOUND]
        valid = pick([int(v) for v in counts]) == 1
        route = pick([v[0] for v in entries])
        which = pick([v[1] for v in entries])
        source_alpha = flipped(alpha, alpha_bits, route // 16)
        source_chip = flipped(chip, chip_bits, route % 16)
        home = jnp.logical_and(source_chip == alpha, source_alpha == chip)
        ins.append((valid, which, source_chip, source_alpha, home))

    barrier = pltpu.get_barrier_semaphore()

    def greet(to_alpha, to_beta):
        pl.semaphore_signal(
            barrier, inc=1, device_id=(to_alpha, to_beta), device_id_type=MESH
        )

    for to_beta in (right + core, left + core, sibling, far):
        greet(alpha, to_beta)
    expected = jnp.int32(4)
    for valid, _, to_alpha, to_chip, home in ins:

        @pl.when(valid)
        def _():
            greet(to_chip, 2 * to_alpha + core)

        expected = expected + jnp.where(valid, jnp.where(home, 1, 2), 0)

    @pl.when(jnp.logical_not(stays))
    def _():
        for to_alpha, to_chip in back:
            greet(to_alpha, 2 * to_chip + 1 - core)
            same = jnp.logical_and(to_alpha == alpha, to_chip == chip)

            @pl.when(jnp.logical_not(same))
            def _():
                greet(to_alpha, 2 * to_chip + core)

    expected = expected + jnp.where(stays, 0, SPREAD)

    def remote(step, kind, i, src_slot, dst_slot, to):
        at = pl.ds(pl.multiple_of(i * chunk_rows, chunk_rows), chunk_rows)
        return pltpu.make_async_remote_copy(
            halo.at[step, src_slot, at],
            halo.at[step, dst_slot, at],
            hsend.at[step, kind, i],
            hrecv.at[step, kind, i],
            device_id=(alpha, to),
            device_id_type=MESH,
        )

    def to_right(step, i):
        return remote(step, 0, i, 3, 1, right + core)

    def to_left(step, i):
        return remote(step, 1, i, 3, 5, left + core)

    def to_sibling(step, i):
        return remote(step, 2, i, 3, 2 * core + 2, sibling)

    def pass_left_tile(step, i):
        return remote(step, 3, i, 1, 2 * core, sibling)

    def pass_right_tile(step, i):
        return remote(step, 4, i, 5, 2 * core + 4, sibling)

    def pass_far(step, i):
        return remote(step, 5, i, 5 - 4 * core, 6 - 6 * core, far)

    halo_kinds = (to_right, to_left, to_sibling, pass_left_tile, pass_right_tile, pass_far)

    def start_own(step, i):
        to_right(step, i).start()
        to_left(step, i).start()
        to_sibling(step, i).start()

    for i in range(CHUNKS):
        load(i).wait()
        at = pl.ds(i * chunk_rows, chunk_rows)
        halo[0, HOPS, at, :] = cur[at, :].astype(jnp.bfloat16)
        if i == 0:
            pl.semaphore_wait(barrier, expected)
        start_own(0, i)

    coup_copy().wait()
    coup[blocks, 0] = jnp.zeros((BLK, BLK), jnp.bfloat16)
    total = blocks * lax.axis_size("beta")
    for j in range(blocks):
        mine = beta * blocks + j
        for t in range(couple):
            offset = (idx_ref[j, t] - mine + REACH + total) % total - REACH
            pos_ref[j, t] = HOPS * blocks + j + offset

    def build(slot, carry):
        for u in range(blocks):
            place = slot * blocks + u
            for j in range(blocks):
                found_j = blocks
                found_t = 0
                for t in range(couple):
                    hit = pos_ref[j, t] == place
                    found_j = jnp.where(hit, j, found_j)
                    found_t = jnp.where(hit, t, found_t)
                banded[slot, pl.ds(u * BLK, BLK), pl.ds(j * BLK, BLK)] = coup[found_j, found_t]
        return carry

    lax.fori_loop(0, TILES, build, 0)

    places = lax.broadcasted_iota(jnp.int32, energy_ref.shape, 0) * BLK + lax.broadcasted_iota(
        jnp.int32, energy_ref.shape, 1
    )

    def shift_of(step):
        chosen = jnp.where(places == shift_ref[step], energy_ref[...], 0.0)
        return 2.0 * jnp.sum(chosen)

    row_blocks = rows // BLK

    def fill_weight(step, shift):
        def body(i, carry):
            row_line = energy_ref[pl.ds(alpha * row_blocks + i, 1), :]
            column = jnp.transpose(jnp.broadcast_to(row_line, (BLK, BLK)))
            at = pl.ds(pl.multiple_of(i * BLK, BLK), BLK)
            for j in range(blocks):
                gap = column + energy_ref[pl.ds(beta * blocks + j, 1), :] - shift
                weight[at, pl.ds(j * BLK, BLK)] = gap / (gap * gap + 1.0)
            return carry

        lax.fori_loop(0, row_blocks, body, 0)

    def leg1(step, p):
        to_alpha, to_beta, slot = outs[p]
        return pltpu.make_async_remote_copy(
            mixed.at[step, :, p],
            inter.at[step, slot],
            leg1_send.at[step, p],
            leg1_recv.at[step, slot],
            device_id=(to_alpha, to_beta),
            device_id_type=MESH,
        )

    def leg1_arrived(step, n):
        return pltpu.make_async_copy(
            inter.at[step, n], inter.at[step, n], leg1_recv.at[step, n]
        )

    def leg2(step, n, to_core):
        _, which, to_alpha, to_chip, _ = ins[n]
        return pltpu.make_async_remote_copy(
            inter.at[step, n, to_core],
            fin.at[step, core, which],
            leg2_send.at[step, n, to_core],
            leg2_recv.at[step, core],
            device_id=(to_alpha, 2 * to_chip + to_core),
            device_id_type=MESH,
        )

    def leg2_self(step, n):
        return pltpu.make_async_copy(
            inter.at[step, n, core], fin.at[step, core, ins[n][1]], leg2_recv.at[step, core]
        )

    def leg0_sibling(step):
        return pltpu.make_async_remote_copy(
            mixed.at[step, 1 - core],
            fin.at[step, core],
            leg1_send.at[step, 0],
            leg2_recv.at[step, core],
            device_id=(alpha, sibling),
            device_id_type=MESH,
        )

    def leg0_self(step):
        return pltpu.make_async_copy(
            mixed.at[step, core], fin.at[step, core], leg2_recv.at[step, core]
        )

    for step in range(STEPS):
        shift = shift_of(step)
        fill_weight(step, shift)

        def forward(i, carry):
            to_right(step, i).wait_recv()
            pass_left_tile(step, i).start()
            to_left(step, i).wait_recv()
            pass_right_tile(step, i).start()
            pass_far(step, i).start()
            return carry

        lax.fori_loop(0, CHUNKS, forward, 0)

        def mix(i, carry):
            for copy in halo_kinds[2:]:
                copy(step, i).wait_recv()
            at = pl.ds(pl.multiple_of(i * chunk_rows, chunk_rows), chunk_rows)
            acc = jnp.dot(halo[step, 0, at, :], banded[0], preferred_element_type=jnp.float32)
            for slot in range(1, TILES):
                acc = acc + jnp.dot(
                    halo[step, slot, at, :], banded[slot], preferred_element_type=jnp.float32
                )
            low = acc.astype(jnp.bfloat16)
            per_half = CHUNKS // 2
            flat = mixed.at[step, i // per_half]
            base = (i % per_half) * chunk_rows
            for q in range(chunk_rows // 16):
                start = base + q * 16
                flat[start // piece, pl.ds(pl.multiple_of(start % piece, 16), 16), :] = low[
                    q * 16 : (q + 1) * 16
                ]
            wide = low.astype(jnp.float32)
            factor = weight[at, :]
            cur[at, :] = cur[at, :] * (1.0 + shift * factor) - wide * factor
            return carry

        lax.fori_loop(0, CHUNKS, mix, 0)

        @pl.when(stays)
        def _():
            leg0_sibling(step).start()
            leg0_self(step).start()

        @pl.when(jnp.logical_not(stays))
        def _():
            for p in range(SPREAD):
                leg1(step, p).start()

        for n in range(INSLOTS):
            valid, home = ins[n][0], ins[n][4]

            @pl.when(valid)
            def _():
                leg1_arrived(step, n).wait()
                leg2(step, n, 1 - core).start()
                pl.when(home)(leg2_self(step, n).start)
                pl.when(jnp.logical_not(home))(leg2(step, n, core).start)

        for copy in halo_kinds:
            for i in range(CHUNKS):
                copy(step, i).wait_send()
        pl.when(stays)(leg0_sibling(step).wait_send)

        @pl.when(jnp.logical_not(stays))
        def _():
            for p in range(SPREAD):
                leg1(step, p).wait_send()

        per_half = CHUNKS // 2
        for c in range(2):
            pltpu.make_async_copy(fin.at[step, c], fin.at[step, c], leg2_recv.at[step, c]).wait()
            for k in range(blocks):
                row = c * half + k * BLK
                for j in range(blocks):
                    lines = []
                    for q in range(BLK // 16):
                        start = j * BLK + q * 16
                        lines.append(
                            fin[step, c, start // piece, pl.ds(start % piece, 16), pl.ds(k * BLK, BLK)]
                        )
                    block = jnp.concatenate(lines, axis=0).astype(jnp.float32)
                    mirror = jnp.transpose(block)
                    at = (pl.ds(row, BLK), pl.ds(j * BLK, BLK))
                    fresh = cur[at] - mirror * weight[at]
                    if step < STEPS - 1:
                        cur[at] = fresh
                        halo[step + 1, HOPS, pl.ds(row, BLK), pl.ds(j * BLK, BLK)] = fresh.astype(
                            jnp.bfloat16
                        )
                    else:
                        out_ref[at] = fresh
                if step < STEPS - 1:
                    start_own(step + 1, row // chunk_rows)

        for n in range(INSLOTS):
            valid, home = ins[n][0], ins[n][4]

            @pl.when(valid)
            def _():
                leg2(step, n, 1 - core).wait_send()
                pl.when(jnp.logical_not(home))(leg2(step, n, core).wait_send)


def local(amplitudes, coupled_index, coupling_blocks, string_energy, shift_index):
    rows, cols = amplitudes.shape
    blocks = coupled_index.shape[0]
    couple = coupled_index.shape[1]
    half = rows // 2
    piece = half // SPREAD
    energy = string_energy.reshape(-1, BLK)
    in_hbm = pl.BlockSpec(memory_space=pltpu.HBM)
    vmem = pl.BlockSpec(memory_space=pltpu.VMEM)
    smem = pl.BlockSpec(memory_space=pltpu.SMEM)
    dma = pltpu.SemaphoreType.DMA
    return pl.pallas_call(
        kernel,
        out_shape=jax.ShapeDtypeStruct((rows, cols), jnp.float32),
        in_specs=[in_hbm, smem, in_hbm, vmem, smem],
        out_specs=vmem,
        scratch_shapes=[
            pltpu.VMEM((rows, cols), jnp.float32),
            pltpu.VMEM((STEPS, TILES, rows, cols), jnp.bfloat16),
            pltpu.VMEM((blocks + 1, couple, BLK, BLK), jnp.bfloat16),
            pltpu.VMEM((TILES, cols, cols), jnp.bfloat16),
            pltpu.VMEM((rows, cols), jnp.float32),
            pltpu.VMEM((STEPS, 2, SPREAD, piece, cols), jnp.bfloat16),
            pltpu.VMEM((STEPS, INSLOTS, 2, piece, cols), jnp.bfloat16),
            pltpu.VMEM((STEPS, 2, SPREAD, piece, cols), jnp.bfloat16),
            pltpu.SMEM((blocks, couple), jnp.int32),
            dma((CHUNKS,)),
            dma,
            dma((STEPS, 6, CHUNKS)),
            dma((STEPS, 6, CHUNKS)),
            dma((STEPS, SPREAD)),
            dma((STEPS, INSLOTS)),
            dma((STEPS, INSLOTS, 2)),
            dma((STEPS, 2)),
        ],
        compiler_params=pltpu.CompilerParams(
            collective_id=0, has_side_effects=True, vmem_limit_bytes=62 * 1024 * 1024
        ),
        cost_estimate=pl.CostEstimate(
            flops=2 * STEPS * TILES * rows * cols * cols, bytes_accessed=8 << 20, transcendentals=0
        ),
        name="residual_steps",
    )(amplitudes, coupled_index, coupling_blocks, energy, shift_index)


def solution(mesh):
    placed = (P("alpha", "beta"), P("beta", None), P("beta", None, None, None), P(), P())
    return jax.shard_map(
        local, mesh=mesh, in_specs=placed, out_specs=P("alpha", "beta"), check_vma=False
    )
```

```python
import jax
import jax.numpy as jnp
from jax import lax
from jax.experimental import pallas as pl
from jax.experimental.pallas import tpu as pltpu
from jax.sharding import PartitionSpec as P

BLK = 128
REACH = 9
STEPS = 2
HOPS = 3
TILES = 2 * HOPS + 1
CHUNKS = 6
SPREAD = 8
GROUPS = 4
LEGWIN = 4
MESH = pl.DeviceIdType.MESH
ROUTES = (
    (),
    (217, 129, 193, 64, 16, 208, 24, 211),
    (40, 217, 238, 120, 88, 144, 170, 48),
    (248, 104, 187, 114, 48, 51, 128, 216),
    (64, 194, 7, 65, 133, 71, 131, 193),
    (40, 151, 144, 21, 42, 21, 210, 80),
    (184, 144, 254, 56, 232, 72, 24, 120),
    (240, 246, 48, 104, 64, 120, 55, 246),
    (64, 192, 128, 64, 64, 192, 128, 8),
    (216, 128, 88, 1, 193, 128, 64, 192),
    (40, 192, 40, 238, 111, 120, 144, 109),
    (64, 58, 184, 195, 3, 168, 120, 249),
    (135, 216, 75, 5, 10, 137, 4, 129),
    (24, 90, 158, 221, 5, 94, 24, 216),
    (187, 104, 216, 144, 41, 216, 184, 46),
    (128, 63, 171, 7, 128, 190, 56, 192),
)


def inbound_routes():
    groups = []
    slots = {}
    base = 0
    for group in range(GROUPS):
        found = [[] for _ in ROUTES]
        for piece in range(group * SPREAD // GROUPS, (group + 1) * SPREAD // GROUPS):
            for kind, row in enumerate(ROUTES):
                if row:
                    at = kind ^ (row[piece] // 16) ^ (row[piece] % 16)
                    slots[kind, piece] = base + len(found[at])
                    found[at].append((row[piece], piece))
        width = max(len(entries) for entries in found)
        groups.append((base, width, found))
        base += width
    return groups, slots, base


INBOUND, SLOTS, INSLOTS = inbound_routes()


def kernel(
    amp_hbm, idx_ref, coup_hbm, energy_ref, shift_ref, out_ref,
    cur, halo, coup, banded, weight, mixed, inter, fin, partial, pos_ref,
    load_sem, coup_sem, hsend, hrecv, leg1_send, leg1_recv, leg2_send, leg2_recv,
):
    rows, cols = amp_hbm.shape
    chunk_rows = rows // CHUNKS
    half = rows // 2
    piece = half // SPREAD
    per_group = SPREAD // GROUPS
    blocks = cols // BLK
    couple = coup_hbm.shape[1]
    alpha = lax.axis_index("alpha")
    beta = lax.axis_index("beta")
    chip = beta // 2
    core = beta % 2
    chips = lax.axis_size("beta") // 2
    next_chip = (chip + chips + 2 * core - 1) % chips
    ahead = 2 * next_chip + core
    behind = 2 * ((chip + chips + 1 - 2 * core) % chips) + core
    sibling = 2 * chip + 1 - core
    far = 2 * next_chip + 1 - core

    def load(i):
        at = pl.ds(i * chunk_rows, chunk_rows)
        return pltpu.make_async_copy(amp_hbm.at[at], cur.at[at], load_sem.at[i])

    def coup_copy():
        return pltpu.make_async_copy(coup_hbm, coup.at[pl.ds(0, blocks)], coup_sem)

    for i in range(CHUNKS):
        load(i).start()
    coup_copy().start()

    def bits(value):
        return [(value // 2**k) % 2 for k in range(4)]

    alpha_bits, chip_bits = bits(alpha), bits(chip)
    kind = sum((p + q) % 2 * 2**k for k, (p, q) in enumerate(zip(alpha_bits, chip_bits)))
    stays = kind == 0

    def pick(values):
        chosen = jnp.int32(values[0])
        for k in range(1, len(ROUTES)):
            if values[k] != values[0]:
                chosen = jnp.where(kind == k, values[k], chosen)
        return chosen

    def flipped(base, base_bits, flips):
        for k in range(4):
            base = base + (flips // 2**k) % 2 * (2**k * (1 - 2 * base_bits[k]))
        return base

    outs = []
    back = []
    for p in range(SPREAD):
        route = pick([row[p] if row else 0 for row in ROUTES])
        slot = pick([SLOTS.get((k, p), 0) for k in range(len(ROUTES))])
        through = flipped(alpha, alpha_bits, route // 16)
        outs.append((through, 2 * flipped(chip, chip_bits, route % 16) + core, slot))
        back.append((flipped(chip, chip_bits, route // 16), flipped(alpha, alpha_bits, route % 16)))
    ins = []
    for found, n in [(found, n) for _, width, found in INBOUND for n in range(width)]:
        entries = [row[n] if n < len(row) else (0, 0) for row in found]
        valid = pick([int(n < len(row)) for row in found]) == 1
        route = pick([v[0] for v in entries])
        which = pick([v[1] for v in entries])
        source_alpha = flipped(alpha, alpha_bits, route // 16)
        source_chip = flipped(chip, chip_bits, route % 16)
        home = jnp.logical_and(source_chip == alpha, source_alpha == chip)
        ins.append((valid, which, source_chip, source_alpha, home))

    barrier = pltpu.get_barrier_semaphore()

    def greet(to_alpha, to_beta):
        pl.semaphore_signal(
            barrier, inc=1, device_id=(to_alpha, to_beta), device_id_type=MESH
        )

    for to_beta in (ahead, behind, sibling, far):
        greet(alpha, to_beta)
    expected = jnp.int32(4)
    for valid, _, to_alpha, to_chip, home in ins:

        @pl.when(valid)
        def _():
            greet(to_chip, 2 * to_alpha + core)

        expected = expected + jnp.where(valid, jnp.where(home, 1, 2), 0)

    @pl.when(jnp.logical_not(stays))
    def _():
        for to_alpha, to_chip in back:
            greet(to_alpha, 2 * to_chip + 1 - core)
            same = jnp.logical_and(to_alpha == alpha, to_chip == chip)

            @pl.when(jnp.logical_not(same))
            def _():
                greet(to_alpha, 2 * to_chip + core)

    expected = expected + jnp.where(stays, 0, SPREAD)

    def remote(step, kind, i, src_slot, dst_slot, to):
        at = pl.ds(pl.multiple_of(i * chunk_rows, chunk_rows), chunk_rows)
        return pltpu.make_async_remote_copy(
            halo.at[step, src_slot, at],
            halo.at[step, dst_slot, at],
            hsend.at[step, kind, i],
            hrecv.at[step, kind, i],
            device_id=(alpha, to),
            device_id_type=MESH,
        )

    def lead(step, i):
        return remote(step, 0, i, 3, 5 - 4 * core, ahead)

    def trail(step, i):
        return remote(step, 1, i, 3, 1 + 4 * core, behind)

    def to_sibling(step, i):
        return remote(step, 2, i, 3, 2 * core + 2, sibling)

    def pass_lead(step, i):
        return remote(step, 3, i, 5 - 4 * core, 4 - 2 * core, sibling)

    def pass_trail(step, i):
        return remote(step, 4, i, 1 + 4 * core, 6 * core, sibling)

    def pass_far(step, i):
        return remote(step, 5, i, 5 - 4 * core, 6 - 6 * core, far)

    halo_kinds = (lead, trail, to_sibling, pass_lead, pass_trail, pass_far)

    def start_own(step, i):
        lead(step, i).start()
        trail(step, i).start()
        to_sibling(step, i).start()

    for i in range(CHUNKS):
        load(i).wait()
        at = pl.ds(i * chunk_rows, chunk_rows)
        halo[0, HOPS, at, :] = cur[at, :].astype(jnp.bfloat16)
        if i == 0:
            pl.semaphore_wait(barrier, expected)
        start_own(0, i)

    coup_copy().wait()
    coup[blocks, 0] = jnp.zeros((BLK, BLK), jnp.bfloat16)
    total = blocks * lax.axis_size("beta")
    for j in range(blocks):
        mine = beta * blocks + j
        for t in range(couple):
            offset = (idx_ref[j, t] - mine + REACH + total) % total - REACH
            pos_ref[j, t] = HOPS * blocks + j + offset

    def build(slot, carry):
        for u in range(blocks):
            place = slot * blocks + u
            for j in range(blocks):
                found_j = blocks
                found_t = 0
                for t in range(couple):
                    hit = pos_ref[j, t] == place
                    found_j = jnp.where(hit, j, found_j)
                    found_t = jnp.where(hit, t, found_t)
                banded[slot, pl.ds(u * BLK, BLK), pl.ds(j * BLK, BLK)] = coup[found_j, found_t]
        return carry

    lax.fori_loop(0, TILES, build, 0)

    places = lax.broadcasted_iota(jnp.int32, energy_ref.shape, 0) * BLK + lax.broadcasted_iota(
        jnp.int32, energy_ref.shape, 1
    )

    def shift_of(step):
        chosen = jnp.where(places == shift_ref[step], energy_ref[...], 0.0)
        return 2.0 * jnp.sum(chosen)

    row_blocks = rows // BLK

    def fill_weight(step, shift):
        def body(i, carry):
            row_line = energy_ref[pl.ds(alpha * row_blocks + i, 1), :]
            column = jnp.transpose(jnp.broadcast_to(row_line, (BLK, BLK)))
            at = pl.ds(pl.multiple_of(i * BLK, BLK), BLK)
            for j in range(blocks):
                gap = column + energy_ref[pl.ds(beta * blocks + j, 1), :] - shift
                weight[at, pl.ds(j * BLK, BLK)] = gap / (gap * gap + 1.0)
            return carry

        lax.fori_loop(0, row_blocks, body, 0)

    def leg1(step, p):
        to_alpha, to_beta, slot = outs[p]
        return pltpu.make_async_remote_copy(
            mixed.at[step, :, p],
            inter.at[step, slot],
            leg1_send.at[step, p],
            leg1_recv.at[step, slot],
            device_id=(to_alpha, to_beta),
            device_id_type=MESH,
        )

    def leg1_arrived(step, n):
        return pltpu.make_async_copy(
            inter.at[step, n], inter.at[step, n], leg1_recv.at[step, n]
        )

    def leg2(step, n, to_core):
        _, which, to_alpha, to_chip, _ = ins[n]
        return pltpu.make_async_remote_copy(
            inter.at[step, n, to_core],
            fin.at[step, core, which],
            leg2_send.at[step, n, to_core],
            leg2_recv.at[step, core],
            device_id=(to_alpha, 2 * to_chip + to_core),
            device_id_type=MESH,
        )

    def leg2_self(step, n):
        return pltpu.make_async_copy(
            inter.at[step, n, core], fin.at[step, core, ins[n][1]], leg2_recv.at[step, core]
        )

    def leg0_sibling(step):
        return pltpu.make_async_remote_copy(
            mixed.at[step, 1 - core],
            fin.at[step, core],
            leg1_send.at[step, 0],
            leg2_recv.at[step, core],
            device_id=(alpha, sibling),
            device_id_type=MESH,
        )

    def leg0_self(step):
        return pltpu.make_async_copy(
            mixed.at[step, core], fin.at[step, core], leg2_recv.at[step, core]
        )

    for step in range(STEPS):
        shift = shift_of(step)
        fill_weight(step, shift)

        def forward(i, carry):
            lead(step, i).wait_recv()
            pass_far(step, i).start()
            pass_lead(step, i).start()
            return carry

        lax.fori_loop(0, CHUNKS, forward, 0)

        def share(i, carry):
            trail(step, i).wait_recv()
            pass_trail(step, i).start()
            return carry

        lax.fori_loop(0, CHUNKS, share, 0)

        def gather(i, carry):
            for copy in halo_kinds[2:5]:
                copy(step, i).wait_recv()
            at = pl.ds(pl.multiple_of(i * chunk_rows, chunk_rows), chunk_rows)
            acc = None
            for near in range(TILES - 1):
                slot = near + 1 - core
                part = jnp.dot(
                    halo[step, slot, at, :], banded[slot], preferred_element_type=jnp.float32
                )
                acc = part if acc is None else acc + part
            partial[at, :] = acc
            return carry

        lax.fori_loop(0, CHUNKS, gather, 0)

        def mix(i, carry):
            pass_far(step, i).wait_recv()
            at = pl.ds(pl.multiple_of(i * chunk_rows, chunk_rows), chunk_rows)
            slot = (TILES - 1) * core
            acc = partial[at, :] + jnp.dot(
                halo[step, slot, at, :], banded[slot], preferred_element_type=jnp.float32
            )
            low = acc.astype(jnp.bfloat16)
            per_half = CHUNKS // 2
            flat = mixed.at[step, i // per_half]
            base = (i % per_half) * chunk_rows
            for q in range(chunk_rows // 16):
                start = base + q * 16
                flat[start // piece, pl.ds(pl.multiple_of(start % piece, 16), 16), :] = low[
                    q * 16 : (q + 1) * 16
                ]
            partial[at, :] = low.astype(jnp.float32)
            return carry

        lax.fori_loop(0, CHUNKS, mix, 0)

        def rebase(i, carry):
            at = pl.ds(pl.multiple_of(i * chunk_rows, chunk_rows), chunk_rows)
            factor = weight[at, :]
            cur[at, :] = cur[at, :] * (1.0 + shift * factor) - partial[at, :] * factor
            return carry

        def outward(g):
            @pl.when(jnp.logical_not(stays))
            def _():
                for p in range(g * per_group, (g + 1) * per_group):
                    leg1(step, p).start()

        def onward(g):
            base, width, _ = INBOUND[g]
            for n in range(base, base + width):
                valid, home = ins[n][0], ins[n][4]

                @pl.when(valid)
                def _():
                    leg1_arrived(step, n).wait()
                    leg2(step, n, 1 - core).start()
                    pl.when(home)(leg2_self(step, n).start)
                    pl.when(jnp.logical_not(home))(leg2(step, n, core).start)

        for g in range(LEGWIN):
            outward(g)

        @pl.when(stays)
        def _():
            leg0_sibling(step).start()
            leg0_self(step).start()

        lax.fori_loop(0, CHUNKS, rebase, 0)

        for g in range(GROUPS):
            onward(g)
            if g + LEGWIN < GROUPS:
                outward(g + LEGWIN)

        for copy in halo_kinds:
            for i in range(CHUNKS):
                copy(step, i).wait_send()
        pl.when(stays)(leg0_sibling(step).wait_send)

        @pl.when(jnp.logical_not(stays))
        def _():
            for p in range(SPREAD):
                leg1(step, p).wait_send()

        per_half = CHUNKS // 2
        for c in range(2):
            pltpu.make_async_copy(fin.at[step, c], fin.at[step, c], leg2_recv.at[step, c]).wait()
            for k in range(blocks):
                row = c * half + k * BLK
                for j in range(blocks):
                    lines = []
                    for q in range(BLK // 16):
                        start = j * BLK + q * 16
                        lines.append(
                            fin[step, c, start // piece, pl.ds(start % piece, 16), pl.ds(k * BLK, BLK)]
                        )
                    block = jnp.concatenate(lines, axis=0).astype(jnp.float32)
                    mirror = jnp.transpose(block)
                    at = (pl.ds(row, BLK), pl.ds(j * BLK, BLK))
                    fresh = cur[at] - mirror * weight[at]
                    if step < STEPS - 1:
                        cur[at] = fresh
                        halo[step + 1, HOPS, pl.ds(row, BLK), pl.ds(j * BLK, BLK)] = fresh.astype(
                            jnp.bfloat16
                        )
                    else:
                        out_ref[at] = fresh
                if step < STEPS - 1:
                    start_own(step + 1, row // chunk_rows)

        for n in range(INSLOTS):
            valid, home = ins[n][0], ins[n][4]

            @pl.when(valid)
            def _():
                leg2(step, n, 1 - core).wait_send()
                pl.when(jnp.logical_not(home))(leg2(step, n, core).wait_send)


def local(amplitudes, coupled_index, coupling_blocks, string_energy, shift_index):
    rows, cols = amplitudes.shape
    blocks = coupled_index.shape[0]
    couple = coupled_index.shape[1]
    half = rows // 2
    piece = half // SPREAD
    energy = string_energy.reshape(-1, BLK)
    in_hbm = pl.BlockSpec(memory_space=pltpu.HBM)
    vmem = pl.BlockSpec(memory_space=pltpu.VMEM)
    smem = pl.BlockSpec(memory_space=pltpu.SMEM)
    dma = pltpu.SemaphoreType.DMA
    return pl.pallas_call(
        kernel,
        out_shape=jax.ShapeDtypeStruct((rows, cols), jnp.float32),
        in_specs=[in_hbm, smem, in_hbm, vmem, smem],
        out_specs=vmem,
        scratch_shapes=[
            pltpu.VMEM((rows, cols), jnp.float32),
            pltpu.VMEM((STEPS, TILES, rows, cols), jnp.bfloat16),
            pltpu.VMEM((blocks + 1, couple, BLK, BLK), jnp.bfloat16),
            pltpu.VMEM((TILES, cols, cols), jnp.bfloat16),
            pltpu.VMEM((rows, cols), jnp.float32),
            pltpu.VMEM((STEPS, 2, SPREAD, piece, cols), jnp.bfloat16),
            pltpu.VMEM((STEPS, INSLOTS, 2, piece, cols), jnp.bfloat16),
            pltpu.VMEM((STEPS, 2, SPREAD, piece, cols), jnp.bfloat16),
            pltpu.VMEM((rows, cols), jnp.float32),
            pltpu.SMEM((blocks, couple), jnp.int32),
            dma((CHUNKS,)),
            dma,
            dma((STEPS, 6, CHUNKS)),
            dma((STEPS, 6, CHUNKS)),
            dma((STEPS, SPREAD)),
            dma((STEPS, INSLOTS)),
            dma((STEPS, INSLOTS, 2)),
            dma((STEPS, 2)),
        ],
        compiler_params=pltpu.CompilerParams(
            collective_id=0, has_side_effects=True, vmem_limit_bytes=62 * 1024 * 1024
        ),
        cost_estimate=pl.CostEstimate(
            flops=2 * STEPS * TILES * rows * cols * cols, bytes_accessed=8 << 20, transcendentals=0
        ),
        name="residual_steps",
    )(amplitudes, coupled_index, coupling_blocks, energy, shift_index)


def solution(mesh):
    placed = (P("alpha", "beta"), P("beta", None), P("beta", None, None, None), P(), P())
    return jax.shard_map(
        local, mesh=mesh, in_specs=placed, out_specs=P("alpha", "beta"), check_vma=False
    )
```

```python
import jax
import jax.numpy as jnp
from jax import lax
from jax.experimental import pallas as pl
from jax.experimental.pallas import tpu as pltpu
from jax.sharding import PartitionSpec as P

BLK = 128
REACH = 9
STEPS = 2
HOPS = 3
TILES = 2 * HOPS + 1
CHUNKS = 6
SPREAD = 8
GROUPS = 4
LEGWIN = 4
MESH = pl.DeviceIdType.MESH
ROUTES = (
    (),
    (217, 129, 193, 64, 16, 208, 24, 211),
    (40, 217, 238, 120, 88, 144, 170, 48),
    (248, 104, 187, 114, 48, 51, 128, 216),
    (64, 194, 7, 65, 133, 71, 131, 193),
    (40, 151, 144, 21, 42, 21, 210, 80),
    (184, 144, 254, 56, 232, 72, 24, 120),
    (240, 246, 48, 104, 64, 120, 55, 246),
    (64, 192, 128, 64, 64, 192, 128, 8),
    (216, 128, 88, 1, 193, 128, 64, 192),
    (40, 192, 40, 238, 111, 120, 144, 109),
    (64, 58, 184, 195, 3, 168, 120, 249),
    (135, 216, 75, 5, 10, 137, 4, 129),
    (24, 90, 158, 221, 5, 94, 24, 216),
    (187, 104, 216, 144, 41, 216, 184, 46),
    (128, 63, 171, 7, 128, 190, 56, 192),
)


def inbound_routes():
    groups = []
    slots = {}
    base = 0
    for group in range(GROUPS):
        found = [[] for _ in ROUTES]
        for piece in range(group * SPREAD // GROUPS, (group + 1) * SPREAD // GROUPS):
            for kind, row in enumerate(ROUTES):
                if row:
                    at = kind ^ (row[piece] // 16) ^ (row[piece] % 16)
                    slots[kind, piece] = base + len(found[at])
                    found[at].append((row[piece], piece))
        width = max(len(entries) for entries in found)
        groups.append((base, width, found))
        base += width
    return groups, slots, base


INBOUND, SLOTS, INSLOTS = inbound_routes()


def kernel(
    amp_hbm, idx_ref, coup_hbm, energy_ref, shift_ref, out_ref,
    cur, halo, coup, banded, weight, mixed, inter, fin, partial, pos_ref,
    load_sem, store_sem, coup_sem, hsend, hrecv, leg1_send, leg1_recv, leg2_send, leg2_recv,
):
    rows, cols = amp_hbm.shape
    chunk_rows = rows // CHUNKS
    half = rows // 2
    piece = half // SPREAD
    per_group = SPREAD // GROUPS
    blocks = cols // BLK
    couple = coup_hbm.shape[1]
    alpha = lax.axis_index("alpha")
    beta = lax.axis_index("beta")
    chip = beta // 2
    core = beta % 2
    chips = lax.axis_size("beta") // 2
    next_chip = (chip + chips + 2 * core - 1) % chips
    ahead = 2 * next_chip + core
    behind = 2 * ((chip + chips + 1 - 2 * core) % chips) + core
    sibling = 2 * chip + 1 - core
    far = 2 * next_chip + 1 - core

    def load(i):
        at = pl.ds(i * chunk_rows, chunk_rows)
        return pltpu.make_async_copy(amp_hbm.at[at], cur.at[at], load_sem.at[i])

    def store(k):
        at = pl.ds(k * BLK, BLK)
        return pltpu.make_async_copy(cur.at[at], out_ref.at[at], store_sem.at[k])

    def coup_copy():
        return pltpu.make_async_copy(coup_hbm, coup.at[pl.ds(0, blocks)], coup_sem)

    for i in range(CHUNKS):
        load(i).start()
    coup_copy().start()

    def bits(value):
        return [(value // 2**k) % 2 for k in range(4)]

    alpha_bits, chip_bits = bits(alpha), bits(chip)
    kind = sum((p + q) % 2 * 2**k for k, (p, q) in enumerate(zip(alpha_bits, chip_bits)))
    stays = kind == 0

    def pick(values):
        chosen = jnp.int32(values[0])
        for k in range(1, len(ROUTES)):
            if values[k] != values[0]:
                chosen = jnp.where(kind == k, values[k], chosen)
        return chosen

    def flipped(base, base_bits, flips):
        for k in range(4):
            base = base + (flips // 2**k) % 2 * (2**k * (1 - 2 * base_bits[k]))
        return base

    outs = []
    back = []
    for p in range(SPREAD):
        route = pick([row[p] if row else 0 for row in ROUTES])
        slot = pick([SLOTS.get((k, p), 0) for k in range(len(ROUTES))])
        through = flipped(alpha, alpha_bits, route // 16)
        outs.append((through, 2 * flipped(chip, chip_bits, route % 16) + core, slot))
        back.append((flipped(chip, chip_bits, route // 16), flipped(alpha, alpha_bits, route % 16)))
    ins = []
    for found, n in [(found, n) for _, width, found in INBOUND for n in range(width)]:
        entries = [row[n] if n < len(row) else (0, 0) for row in found]
        valid = pick([int(n < len(row)) for row in found]) == 1
        route = pick([v[0] for v in entries])
        which = pick([v[1] for v in entries])
        source_alpha = flipped(alpha, alpha_bits, route // 16)
        source_chip = flipped(chip, chip_bits, route % 16)
        home = jnp.logical_and(source_chip == alpha, source_alpha == chip)
        ins.append((valid, which, source_chip, source_alpha, home))

    barrier = pltpu.get_barrier_semaphore()

    def greet(to_alpha, to_beta):
        pl.semaphore_signal(
            barrier, inc=1, device_id=(to_alpha, to_beta), device_id_type=MESH
        )

    for to_beta in (ahead, behind, sibling, far):
        greet(alpha, to_beta)
    expected = jnp.int32(4)
    for valid, _, to_alpha, to_chip, home in ins:

        @pl.when(valid)
        def _():
            greet(to_chip, 2 * to_alpha + core)

        expected = expected + jnp.where(valid, jnp.where(home, 1, 2), 0)

    @pl.when(jnp.logical_not(stays))
    def _():
        for to_alpha, to_chip in back:
            greet(to_alpha, 2 * to_chip + 1 - core)
            same = jnp.logical_and(to_alpha == alpha, to_chip == chip)

            @pl.when(jnp.logical_not(same))
            def _():
                greet(to_alpha, 2 * to_chip + core)

    expected = expected + jnp.where(stays, 0, SPREAD)

    def remote(step, kind, i, src_slot, dst_slot, to):
        at = pl.ds(pl.multiple_of(i * chunk_rows, chunk_rows), chunk_rows)
        return pltpu.make_async_remote_copy(
            halo.at[step, src_slot, at],
            halo.at[step, dst_slot, at],
            hsend.at[step, kind, i],
            hrecv.at[step, kind, i],
            device_id=(alpha, to),
            device_id_type=MESH,
        )

    def lead(step, i):
        return remote(step, 0, i, 3, 5 - 4 * core, ahead)

    def trail(step, i):
        return remote(step, 1, i, 3, 1 + 4 * core, behind)

    def to_sibling(step, i):
        return remote(step, 2, i, 3, 2 * core + 2, sibling)

    def pass_lead(step, i):
        return remote(step, 3, i, 5 - 4 * core, 4 - 2 * core, sibling)

    def pass_trail(step, i):
        return remote(step, 4, i, 1 + 4 * core, 6 * core, sibling)

    def pass_far(step, i):
        return remote(step, 5, i, 5 - 4 * core, 6 - 6 * core, far)

    halo_kinds = (lead, trail, to_sibling, pass_lead, pass_trail, pass_far)

    def start_own(step, i):
        lead(step, i).start()
        trail(step, i).start()
        to_sibling(step, i).start()

    for i in range(CHUNKS):
        load(i).wait()
        at = pl.ds(i * chunk_rows, chunk_rows)
        halo[0, HOPS, at, :] = cur[at, :].astype(jnp.bfloat16)
        if i == 0:
            pl.semaphore_wait(barrier, expected)
        start_own(0, i)

    coup_copy().wait()
    coup[blocks, 0] = jnp.zeros((BLK, BLK), jnp.bfloat16)
    total = blocks * lax.axis_size("beta")
    for j in range(blocks):
        mine = beta * blocks + j
        for t in range(couple):
            offset = (idx_ref[j, t] - mine + REACH + total) % total - REACH
            pos_ref[j, t] = HOPS * blocks + j + offset

    def build(slot, carry):
        for u in range(blocks):
            place = slot * blocks + u
            for j in range(blocks):
                found_j = blocks
                found_t = 0
                for t in range(couple):
                    hit = pos_ref[j, t] == place
                    found_j = jnp.where(hit, j, found_j)
                    found_t = jnp.where(hit, t, found_t)
                banded[slot, pl.ds(u * BLK, BLK), pl.ds(j * BLK, BLK)] = coup[found_j, found_t]
        return carry

    lax.fori_loop(0, TILES, build, 0)

    places = lax.broadcasted_iota(jnp.int32, energy_ref.shape, 0) * BLK + lax.broadcasted_iota(
        jnp.int32, energy_ref.shape, 1
    )

    def shift_of(step):
        chosen = jnp.where(places == shift_ref[step], energy_ref[...], 0.0)
        return 2.0 * jnp.sum(chosen)

    row_blocks = rows // BLK

    def fill_weight(step, shift):
        def body(i, carry):
            row_line = energy_ref[pl.ds(alpha * row_blocks + i, 1), :]
            column = jnp.transpose(jnp.broadcast_to(row_line, (BLK, BLK)))
            at = pl.ds(pl.multiple_of(i * BLK, BLK), BLK)
            for j in range(blocks):
                gap = column + energy_ref[pl.ds(beta * blocks + j, 1), :] - shift
                weight[at, pl.ds(j * BLK, BLK)] = gap / (gap * gap + 1.0)
            return carry

        lax.fori_loop(0, row_blocks, body, 0)

    def leg1(step, p):
        to_alpha, to_beta, slot = outs[p]
        return pltpu.make_async_remote_copy(
            mixed.at[step, :, p],
            inter.at[step, slot],
            leg1_send.at[step, p],
            leg1_recv.at[step, slot],
            device_id=(to_alpha, to_beta),
            device_id_type=MESH,
        )

    def leg1_arrived(step, n):
        return pltpu.make_async_copy(
            inter.at[step, n], inter.at[step, n], leg1_recv.at[step, n]
        )

    def leg2(step, n, to_core):
        _, which, to_alpha, to_chip, _ = ins[n]
        return pltpu.make_async_remote_copy(
            inter.at[step, n, to_core],
            fin.at[step, core, which],
            leg2_send.at[step, n, to_core],
            leg2_recv.at[step, core],
            device_id=(to_alpha, 2 * to_chip + to_core),
            device_id_type=MESH,
        )

    def leg2_self(step, n):
        return pltpu.make_async_copy(
            inter.at[step, n, core], fin.at[step, core, ins[n][1]], leg2_recv.at[step, core]
        )

    def leg0_sibling(step):
        return pltpu.make_async_remote_copy(
            mixed.at[step, 1 - core],
            fin.at[step, core],
            leg1_send.at[step, 0],
            leg2_recv.at[step, core],
            device_id=(alpha, sibling),
            device_id_type=MESH,
        )

    def leg0_self(step):
        return pltpu.make_async_copy(
            mixed.at[step, core], fin.at[step, core], leg2_recv.at[step, core]
        )

    for step in range(STEPS):
        shift = shift_of(step)
        fill_weight(step, shift)

        def forward(i, carry):
            lead(step, i).wait_recv()
            pass_far(step, i).start()
            pass_lead(step, i).start()
            return carry

        lax.fori_loop(0, CHUNKS, forward, 0)

        def share(i, carry):
            trail(step, i).wait_recv()
            pass_trail(step, i).start()
            return carry

        lax.fori_loop(0, CHUNKS, share, 0)

        def gather(i, carry):
            for copy in halo_kinds[2:5]:
                copy(step, i).wait_recv()
            at = pl.ds(pl.multiple_of(i * chunk_rows, chunk_rows), chunk_rows)
            acc = None
            for near in range(TILES - 1):
                slot = near + 1 - core
                part = jnp.dot(
                    halo[step, slot, at, :], banded[slot], preferred_element_type=jnp.float32
                )
                acc = part if acc is None else acc + part
            partial[at, :] = acc
            return carry

        lax.fori_loop(0, CHUNKS, gather, 0)

        def mix(i, carry):
            pass_far(step, i).wait_recv()
            at = pl.ds(pl.multiple_of(i * chunk_rows, chunk_rows), chunk_rows)
            slot = (TILES - 1) * core
            acc = partial[at, :] + jnp.dot(
                halo[step, slot, at, :], banded[slot], preferred_element_type=jnp.float32
            )
            low = acc.astype(jnp.bfloat16)
            per_half = CHUNKS // 2
            flat = mixed.at[step, i // per_half]
            base = (i % per_half) * chunk_rows
            for q in range(chunk_rows // 16):
                start = base + q * 16
                flat[start // piece, pl.ds(pl.multiple_of(start % piece, 16), 16), :] = low[
                    q * 16 : (q + 1) * 16
                ]
            partial[at, :] = low.astype(jnp.float32)
            return carry

        lax.fori_loop(0, CHUNKS, mix, 0)

        def rebase(i, carry):
            at = pl.ds(pl.multiple_of(i * chunk_rows, chunk_rows), chunk_rows)
            factor = weight[at, :]
            cur[at, :] = cur[at, :] * (1.0 + shift * factor) - partial[at, :] * factor
            return carry

        def outward(g):
            @pl.when(jnp.logical_not(stays))
            def _():
                for p in range(g * per_group, (g + 1) * per_group):
                    leg1(step, p).start()

        def onward(g):
            base, width, _ = INBOUND[g]
            for n in range(base, base + width):
                valid, home = ins[n][0], ins[n][4]

                @pl.when(valid)
                def _():
                    leg1_arrived(step, n).wait()
                    leg2(step, n, 1 - core).start()
                    pl.when(home)(leg2_self(step, n).start)
                    pl.when(jnp.logical_not(home))(leg2(step, n, core).start)

        for g in range(LEGWIN):
            outward(g)

        @pl.when(stays)
        def _():
            leg0_sibling(step).start()
            leg0_self(step).start()

        lax.fori_loop(0, CHUNKS, rebase, 0)

        for g in range(GROUPS):
            onward(g)
            if g + LEGWIN < GROUPS:
                outward(g + LEGWIN)

        for copy in halo_kinds:
            for i in range(CHUNKS):
                copy(step, i).wait_send()
        pl.when(stays)(leg0_sibling(step).wait_send)

        @pl.when(jnp.logical_not(stays))
        def _():
            for p in range(SPREAD):
                leg1(step, p).wait_send()

        per_half = CHUNKS // 2
        for c in range(2):
            pltpu.make_async_copy(fin.at[step, c], fin.at[step, c], leg2_recv.at[step, c]).wait()
            for k in range(blocks):
                row = c * half + k * BLK
                for j in range(blocks):
                    lines = []
                    for q in range(BLK // 16):
                        start = j * BLK + q * 16
                        lines.append(
                            fin[step, c, start // piece, pl.ds(start % piece, 16), pl.ds(k * BLK, BLK)]
                        )
                    block = jnp.concatenate(lines, axis=0).astype(jnp.float32)
                    mirror = jnp.transpose(block)
                    at = (pl.ds(row, BLK), pl.ds(j * BLK, BLK))
                    fresh = cur[at] - mirror * weight[at]
                    cur[at] = fresh
                    if step < STEPS - 1:
                        halo[step + 1, HOPS, pl.ds(row, BLK), pl.ds(j * BLK, BLK)] = fresh.astype(
                            jnp.bfloat16
                        )
                if step < STEPS - 1:
                    start_own(step + 1, row // chunk_rows)
                else:
                    store(row // BLK).start()

        for n in range(INSLOTS):
            valid, home = ins[n][0], ins[n][4]

            @pl.when(valid)
            def _():
                leg2(step, n, 1 - core).wait_send()
                pl.when(jnp.logical_not(home))(leg2(step, n, core).wait_send)

    for k in range(row_blocks):
        store(k).wait()


def local(amplitudes, coupled_index, coupling_blocks, string_energy, shift_index):
    rows, cols = amplitudes.shape
    blocks = coupled_index.shape[0]
    couple = coupled_index.shape[1]
    half = rows // 2
    piece = half // SPREAD
    energy = string_energy.reshape(-1, BLK)
    in_hbm = pl.BlockSpec(memory_space=pltpu.HBM)
    vmem = pl.BlockSpec(memory_space=pltpu.VMEM)
    smem = pl.BlockSpec(memory_space=pltpu.SMEM)
    dma = pltpu.SemaphoreType.DMA
    return pl.pallas_call(
        kernel,
        out_shape=jax.ShapeDtypeStruct((rows, cols), jnp.float32),
        in_specs=[in_hbm, smem, in_hbm, vmem, smem],
        out_specs=in_hbm,
        scratch_shapes=[
            pltpu.VMEM((rows, cols), jnp.float32),
            pltpu.VMEM((STEPS, TILES, rows, cols), jnp.bfloat16),
            pltpu.VMEM((blocks + 1, couple, BLK, BLK), jnp.bfloat16),
            pltpu.VMEM((TILES, cols, cols), jnp.bfloat16),
            pltpu.VMEM((rows, cols), jnp.float32),
            pltpu.VMEM((STEPS, 2, SPREAD, piece, cols), jnp.bfloat16),
            pltpu.VMEM((STEPS, INSLOTS, 2, piece, cols), jnp.bfloat16),
            pltpu.VMEM((STEPS, 2, SPREAD, piece, cols), jnp.bfloat16),
            pltpu.VMEM((rows, cols), jnp.float32),
            pltpu.SMEM((blocks, couple), jnp.int32),
            dma((CHUNKS,)),
            dma((rows // BLK,)),
            dma,
            dma((STEPS, 6, CHUNKS)),
            dma((STEPS, 6, CHUNKS)),
            dma((STEPS, SPREAD)),
            dma((STEPS, INSLOTS)),
            dma((STEPS, INSLOTS, 2)),
            dma((STEPS, 2)),
        ],
        compiler_params=pltpu.CompilerParams(
            collective_id=0, has_side_effects=True, vmem_limit_bytes=62 * 1024 * 1024
        ),
        cost_estimate=pl.CostEstimate(
            flops=2 * STEPS * TILES * rows * cols * cols, bytes_accessed=8 << 20, transcendentals=0
        ),
        name="residual_steps",
    )(amplitudes, coupled_index, coupling_blocks, energy, shift_index)


def solution(mesh):
    placed = (P("alpha", "beta"), P("beta", None), P("beta", None, None, None), P(), P())
    return jax.shard_map(
        local, mesh=mesh, in_specs=placed, out_specs=P("alpha", "beta"), check_vma=False
    )
```
